128 devices in a mesh: row: 4 (over y_lo, core), col: 32 (over z, y_hi, x).
Axes of the slice: x: 4, y: 4 (y_hi: 2, y_lo: 2; y = y_hi * 2 + y_lo), z: 4, core: 2. Of those that a mesh axis runs over, the one named last changes fastest.
Arguments:
- matrix_tiles: float32 [4, 32, 4, 256, 256], P('row', 'col'), as said below
- tile_rows: int32 [4, 32, 4], P('row', 'col'), may hold values from 0 to 7, as said below
- keep_rows: int32 [4, 32, 4], P('row', 'col'), may hold values from 0 to 7, as said below
- owners: int32 [4, 128, 1], P('row', 'col'), may hold values from 0 to 3; in each aligned block of 4 rows (0 to 3, 4 to 7, ..., all dimensions but the last counted through in order) at most 2 rows name the same one
Outputs:
- owned: float32 [4, 32, 8, 256, 256], P('row', 'col')
The draws below stay inside these ranges and needn't reach their ends.
Inputs may be any that keep to these rules, and one draw needn't show every extreme that they name: `matrix_tiles`: every entry is positive. `tile_rows`: for each r and tile column j the 4 entries are distinct, and include j % 8 where j // 8 == r. `keep_rows`: for each r and tile column j the 4 entries are distinct, and include j % 8 where j // 8 == r. `owners`: among the 4 kept tiles of one row block and one column block, at most 2 go to the same owner.
All inputs are finite; a program needn't handle non-finite values.
Results may differ from the reference program's by a relative error of at most 0.000071.
Values sent between devices are 32-bit elements; how exact they have to be, the bound alone decides.
A program may use at most 192 MiB of HBM per device.

```python
import math
import jax
import jax.numpy as jnp
import numpy as np
from jax import lax

TILE = 256
TR = 8
NZ = 4
KEEP = 4
NT = 32
CT = 1
MOST = 2
NORD = 8192
N_ROW = 4
N_COL = 32


def distinct_rows(key, count):
    scores = jax.random.randint(key, (N_ROW, NT, TR), 0, 1 << 20) * TR + jnp.arange(TR, dtype=jnp.int32)
    block_index = jnp.arange(N_ROW, dtype=jnp.int32)[:, None, None]
    column_index = jnp.arange(NT, dtype=jnp.int32)[None, :, None]
    level_index = jnp.arange(TR, dtype=jnp.int32)[None, None, :]
    diagonal = (column_index // TR == block_index) & (column_index % TR == level_index)
    scores = jnp.where(diagonal, -1, scores)
    return jnp.argsort(scores, axis=-1)[..., :count].astype(jnp.int32)


def draw_tile_rows(key, part):
    return distinct_rows(jax.random.fold_in(key, 11), NZ)


def draw_keep_rows(key, part):
    return distinct_rows(jax.random.fold_in(key, 13), KEEP)


def draw_matrix_tiles(key, part):
    shape = (N_ROW, NT, NZ, TILE, TILE)
    first = jax.random.fold_in(jax.random.fold_in(key, 17), 0)
    values = jax.random.uniform(first, shape, jnp.float32, 0.2, 1.8)
    return (values * (1.0 / TILE)).astype(jnp.float32)


def assign_block(rng, own, number, rows, number_of, top, bound, slope):
    sequence = jax.random.permutation(rng, number_of)
    packed, ordinary = load_shares(number_of, rows * top, bound, slope, True), load_shares(number_of, rows * top, bound, slope, False)
    places = jnp.arange(number_of)

    def named(sizes, rotation):
        used = int((sizes > 0).sum())
        fixed = max(1, used // 4)
        passed = fixed + (places - fixed + rotation * (used - fixed)) % max(1, number_of - fixed)
        return jnp.zeros((number_of,), jnp.int32).at[sequence[jnp.where(places < fixed, places, passed)]].set(jnp.asarray(sizes, jnp.int32))

    sizes = jnp.where(number % 4 == 0, named(packed, number // 4), named(ordinary, number - number // 4 - 1))
    mixed = jax.random.permutation(jax.random.fold_in(own, 3), number_of)
    giver, sink = mixed[0:number_of // 2 * 2:2], mixed[1:number_of // 2 * 2:2]
    slack = jnp.minimum(sizes[giver] - 1, bound - sizes[sink]) // 2
    slack = jnp.where((giver == sequence[0]) | (sink == sequence[0]) | (sizes[sink] == 0), 0, jnp.maximum(slack, 0))
    passed = jax.random.randint(jax.random.fold_in(own, 4), (number_of // 2,), 0, 1 << 20) % (slack + 1)
    sizes = sizes.at[giver].add(-passed).at[sink].add(passed)
    items = jnp.searchsorted(jnp.cumsum(sizes), jnp.arange(rows * top), side="right").astype(jnp.int32)
    table = items.reshape(top, rows).T
    table = table[jax.random.permutation(jax.random.fold_in(own, 1), rows)]
    rotation = jax.random.randint(jax.random.fold_in(own, 2), (rows, 1), 0, top)
    return jnp.take_along_axis(table, (jnp.arange(top)[None, :] + rotation) % top, axis=1)


def load_shares(count, total, bound, skew, full):
    loads = [(1 << 20) // math.isqrt(rank ** skew) + 1 for rank in range(1, count + 1)]
    largest = bound if full else min(bound, max(-(-total // count), total * loads[0] // sum(loads)))
    least = 1 if total - largest >= count - 1 else 0
    given, spare = [largest] + [least] * (count - 1), total - largest - least * (count - 1)
    while spare > 0:
        candidates = [i for i in range(1, count) if given[i] < largest] or [i for i in range(1, count) if given[i] < bound]
        mass, left = sum([loads[i] for i in candidates]), spare
        for i in candidates:
            addition = min(bound - given[i], max(1, left * loads[i] // mass), spare)
            given[i] = given[i] + addition
            spare = spare - addition
    return np.array(given)


def setup_inputs(seed: int = 0) -> dict:
    streams_of = jax.random.split(jax.random.key(seed), 5)
    matrix_tiles = draw_matrix_tiles(jax.random.fold_in(streams_of[4], 71), 0)
    tile_rows = draw_tile_rows(jax.random.fold_in(streams_of[4], 71), 0)
    keep_rows = draw_keep_rows(jax.random.fold_in(streams_of[4], 71), 0)
    owners_keys = jax.random.split(jax.random.fold_in(streams_of[3], 1), N_ROW * (NT * KEEP) // (CT * KEEP))
    owners_turns = jax.random.permutation(jax.random.fold_in(streams_of[3], 3), N_ROW * (NT * KEEP) // (CT * KEEP))
    owners = jax.vmap(lambda own, number: assign_block(jax.random.fold_in(streams_of[3], 2), own, number, CT * KEEP, N_ROW, 1, MOST, 2))(owners_keys, owners_turns).reshape((N_ROW, NT * KEEP, 1))
    return {"matrix_tiles": matrix_tiles, "tile_rows": tile_rows, "keep_rows": keep_rows, "owners": owners}


def reference(matrix_tiles, tile_rows, keep_rows, owners):
    highest = lax.Precision.HIGHEST
    levels = jnp.arange(TR, dtype=jnp.int32)
    selector = (tile_rows[..., None] == levels).astype(jnp.float32)
    dense = jnp.einsum("rjzl,rjzab->rlajb", selector, matrix_tiles.astype(jnp.float32), precision=highest)
    dense = dense.reshape(NORD, NORD)
    expanded = jnp.dot(dense, dense, precision=highest, preferred_element_type=jnp.float32)
    grid = expanded.reshape(NT, TILE, NT, TILE)
    global_rows = jnp.arange(N_ROW, dtype=jnp.int32)[:, None, None] * TR + keep_rows.astype(jnp.int32)
    columns = jnp.arange(NT, dtype=jnp.int32)[None, :, None]
    kept = grid[global_rows, :, columns, :]
    inflated = kept * kept
    column_total = jnp.sum(inflated, axis=(0, 2, 3))
    normalized = NORD * inflated / column_total[None, :, None, None, :]
    items = CT * KEEP
    values = normalized.reshape(N_ROW, N_COL, items, TILE, TILE)
    targets = owners.reshape(N_ROW, N_COL, items).astype(jnp.int32)
    order = jnp.arange(items, dtype=jnp.int32)
    earlier = jnp.sum(((targets[..., None, :] == targets[..., :, None]) & (order[None, :] < order[:, None])).astype(jnp.int32), axis=-1)
    dest_hit = (targets[..., None] == jnp.arange(N_ROW, dtype=jnp.int32))[..., None]
    slot_hit = (earlier[..., None] == jnp.arange(MOST, dtype=jnp.int32))[..., None, :]
    placing = (dest_hit & slot_hit).astype(jnp.float32)
    owned = jnp.einsum("rcfdn,rcfab->dcrnab", placing, values, precision=highest)
    return owned.reshape(N_ROW, N_COL, N_ROW * MOST, TILE, TILE)
```

```python
import functools

import jax
import jax.numpy as jnp
from jax import lax
from jax.experimental import pallas as pl
from jax.experimental.pallas import tpu as pltpu
from jax.sharding import PartitionSpec as P

MESH = pl.DeviceIdType.MESH
TILE = 256
TR = 8
CHUNKS = 4
ROWS = TILE // CHUNKS
PIECES = 2
DONE = 32


class Copies:
    def __init__(self, send_sems, recv_sems):
        self.send_sems, self.recv_sems, self.made = send_sems, recv_sems, []

    def start(self, src, dst, device):
        number = len(self.made)
        copy = pltpu.make_async_remote_copy(
            src_ref=src,
            dst_ref=dst,
            send_sem=self.send_sems.at[number],
            recv_sem=self.recv_sems.at[number],
            device_id=device,
            device_id_type=MESH,
        )
        copy.start()
        self.made.append(copy)
        return copy

    def finish(self):
        for copy in self.made:
            copy.wait_send()


REMOTE = 3 + 7 + 3 + PIECES * (3 + 3 + 4) + CHUNKS * (9 + 4 + 3) + 3
LOCAL = 1 + CHUNKS + PIECES * 2 + 2


def kernel(
    tiles, meta, owners, out, totals,
    plane_meta, column_meta, plane_scalars, column_scalars, places,
    a_land, a_hi, a_lo, b_own, b_land, b_hi, b_lo,
    partial, far, near, inflated, outgoing, sums,
    send_sems, recv_sems, local_sems,
):
    row, col = lax.axis_index("row"), lax.axis_index("col")
    yl, core = row // 2, row % 2
    z, yh, x = col // 8, (col // 4) % 2, col % 4
    mine = yh * 4 + x

    def in_plane(dy, dx):
        return (row, z * 8 + ((yh + dy) % 2) * 4 + (x + dx) % 4)

    def in_row(dyl, dc):
        return (((yl + dyl) % 2) * 2 + (core + dc) % 2, col)

    def in_z(d):
        return (row, ((z + d) % 4) * 8 + mine)

    plane = [(dy, dx) for dy in range(2) for dx in range(4) if (dy, dx) != (0, 0)]
    rows = [(0, 1), (1, 0), (1, 1)]
    partners = [in_plane(*p) for p in plane] + [in_row(*p) for p in rows] + [in_z(d) for d in (1, 2, 3)]
    barrier = pltpu.get_barrier_semaphore()
    for device in partners:
        pl.semaphore_signal(barrier, inc=1, device_id=device, device_id_type=MESH)
    pl.semaphore_wait(barrier, len(partners))

    copies = Copies(send_sems, recv_sems)
    local_count = [0]

    def local(src, dst):
        copy = pltpu.make_async_copy(src, dst, local_sems.at[local_count[0]])
        local_count[0] += 1
        copy.start()
        return copy

    right, left, across = in_plane(0, 1), in_plane(0, 3), in_plane(1, 0)
    b_right, b_left = yh * 4 + (x + 1) % 4, yh * 4 + (x + 3) % 4
    b_across = (1 - yh) * 4 + x
    b_across_right, b_across_left = (1 - yh) * 4 + (x + 1) % 4, (1 - yh) * 4 + (x + 3) % 4

    def chunk(h):
        return pl.ds(h * ROWS, ROWS)

    a = [dict() for _ in range(CHUNKS)]

    def a_own(h):
        src = tiles.at[:, chunk(h)]
        a[h]["right"] = copies.start(src, a_land.at[h, mine], right)
        a[h]["left"] = copies.start(src, a_land.at[h, mine], left)
        a[h]["across"] = copies.start(src, a_land.at[h, mine], across)
        a[h]["self"] = local(src, a_land.at[h, mine])

    def a_pass_own(h):
        a[h]["right"].wait_recv()
        block = a_land.at[h, b_left, pl.ds(0, 2)]
        a[h]["right2"] = copies.start(block, block, right)
        a[h]["left"].wait_recv()
        block = a_land.at[h, b_right, pl.ds(2, 2)]
        a[h]["left2"] = copies.start(block, block, left)

    def a_across(h):
        a[h]["across"].wait_recv()
        block = a_land.at[h, b_across]
        a[h]["aright"] = copies.start(block, block, right)
        a[h]["aleft"] = copies.start(block, block, left)

    def a_pass_across(h):
        a[h]["aright"].wait_recv()
        block = a_land.at[h, b_across_left, pl.ds(0, 2)]
        a[h]["aright2"] = copies.start(block, block, right)
        a[h]["aleft"].wait_recv()
        block = a_land.at[h, b_across_right, pl.ds(2, 2)]
        a[h]["aleft2"] = copies.start(block, block, left)

    def a_ready(h):
        a[h]["self"].wait()
        for name in ("right2", "left2", "aright2", "aleft2"):
            a[h][name].wait_recv()

    own_meta = local(meta, column_meta.at[z, row])
    meta_row = [copies.start(meta, column_meta.at[z, row], in_row(*p)) for p in rows]
    meta_plane = [copies.start(meta, plane_meta.at[mine], in_plane(*p)) for p in plane]
    plane_meta[mine] = meta[...]
    a_own(0)

    b_row, b_self = [], []
    for p in range(PIECES):
        step = 2 // PIECES
        piece = pl.ds(p * step, step)
        b_row.append([
            copies.start(
                tiles.at[pl.ds(2 * ((core + dc) % 2) + p * step, step)],
                b_own.at[row, piece],
                in_row(dyl, dc),
            )
            for dyl, dc in rows
        ])
        b_self.append(local(tiles.at[pl.ds(2 * core + p * step, step)], b_own.at[row, piece]))
    if CHUNKS > 1:
        a_own(1)

    own_meta.wait()
    for copy in meta_row:
        copy.wait_recv()
    meta_z = [copies.start(column_meta.at[z], column_meta.at[z], in_z(d)) for d in (1, 2, 3)]

    a_pass_own(0)
    a_across(0)
    b_z, b_here = [], []
    for p in range(PIECES):
        step = 2 // PIECES
        piece = pl.ds(p * step, step)
        place = pl.ds(2 * core + p * step, step)
        for copy in b_row[p]:
            copy.wait_recv()
        b_self[p].wait()
        b_z.append([
            copies.start(b_own.at[(z + d) % 4, piece], b_land.at[z, place], in_z(d)) for d in (1, 3, 2)
        ])
        b_here.append(local(b_own.at[z, piece], b_land.at[z, place]))
        if p == 0:
            a_pass_across(0)

    for copy in meta_plane + meta_z:
        copy.wait_recv()
    to_scalars = [local(plane_meta, plane_scalars), local(column_meta, column_scalars)]
    for copy in to_scalars:
        copy.wait()
    for d in range(4):
        zc = (z + d) % 4
        for slot in range(4):
            level = column_scalars[zc, z, 0, slot]
            for m in range(4):
                keep = column_scalars[zc, row, 0, 4 + m]
                place = jnp.int32(DONE)
                for t in range(4):
                    found = plane_scalars[level, 0, t] == keep
                    place = jnp.where(found, level * 4 + t, place)
                places[(d * 4 + slot) * 4 + m] = place

    if CHUNKS > 1:
        a_pass_own(1)
        a_across(1)

    b_share = []
    for p in range(PIECES):
        step = 2 // PIECES
        place = pl.ds(2 * core + p * step, step)
        b_here[p].wait()
        block = b_land.at[z, place]
        b_share.append(copies.start(block, block, in_row(0, 1)))
        for copy, d in zip(b_z[p], (1, 3, 2)):
            copy.wait_recv()
            block = b_land.at[(z + 4 - d) % 4, place]
            b_share.append(copies.start(block, block, in_row(0, 1)))
    for copy in b_share:
        copy.wait_recv()
    for d in range(4):
        for slot in range(4):
            value = b_land[(z + d) % 4, slot]
            high = value.astype(jnp.bfloat16)
            b_hi[d * 4 + slot] = high
            b_lo[d * 4 + slot] = (value - high.astype(jnp.float32)).astype(jnp.bfloat16)
    a_hi[DONE] = jnp.zeros((ROWS, TILE), jnp.bfloat16)
    a_lo[DONE] = jnp.zeros((ROWS, TILE), jnp.bfloat16)
    inflated[4] = jnp.zeros((ROWS, TILE), jnp.float32)

    def products(h, d):
        total = jnp.zeros((4 * ROWS, TILE), jnp.float32)
        for slot in range(4):
            where = [places[(d * 4 + slot) * 4 + m] for m in range(4)]
            high = jnp.concatenate([a_hi[w] for w in where], axis=0)
            low = jnp.concatenate([a_lo[w] for w in where], axis=0)
            right_high, right_low = b_hi[d * 4 + slot], b_lo[d * 4 + slot]
            total += jnp.dot(high, right_high, preferred_element_type=jnp.float32)
            total += jnp.dot(low, right_high, preferred_element_type=jnp.float32)
            total += jnp.dot(high, right_low, preferred_element_type=jnp.float32)
        partial[h, d] = total.reshape(4, ROWS, TILE)

    column_sum = jnp.zeros((8, TILE), jnp.float32)
    slots = []
    for owner in range(4):
        first, second = jnp.int32(4), jnp.int32(4)
        for m in (3, 2, 1, 0):
            hit = owners[m] == owner
            second = jnp.where(hit, first, second)
            first = jnp.where(hit, m, first)
        slots += [first, second]

    sent_out = []
    for h in range(CHUNKS):
        a_ready(h)
        for b in range(TR):
            for t in range(4):
                value = a_land[h, b, t]
                high = value.astype(jnp.bfloat16)
                a_hi[b * 4 + t] = high
                a_lo[b * 4 + t] = (value - high.astype(jnp.float32)).astype(jnp.bfloat16)
        products(h, 2)
        far_up = copies.start(partial.at[h, 2, pl.ds(0, 2)], far.at[h, 0], in_z(1))
        far_down = copies.start(partial.at[h, 2, pl.ds(2, 2)], far.at[h, 1], in_z(3))
        if h + 1 < CHUNKS:
            a_pass_across(h + 1)
        products(h, 1)
        products(h, 3)
        if h + 2 < CHUNKS:
            a_own(h + 2)
        far_up.wait_recv()
        partial[h, 1, 0:2] = partial[h, 1, 0:2] + far[h, 0]
        near_up = copies.start(partial.at[h, 1], near.at[h, 0], in_z(1))
        far_down.wait_recv()
        partial[h, 3, 2:4] = partial[h, 3, 2:4] + far[h, 1]
        near_down = copies.start(partial.at[h, 3], near.at[h, 1], in_z(3))
        products(h, 0)
        if h + 2 < CHUNKS:
            a_pass_own(h + 2)
            a_across(h + 2)
        near_up.wait_recv()
        near_down.wait_recv()
        for m in range(4):
            value = partial[h, 0, m] + near[h, 0, m] + near[h, 1, m]
            value = value * value
            inflated[m] = value
            column_sum = column_sum + jnp.sum(value.reshape(ROWS // 8, 8, TILE), axis=0)
        for owner in range(4):
            for n in range(2):
                outgoing[h, owner, n] = inflated[slots[owner * 2 + n]]
        for dyl, dc in rows:
            device = in_row(dyl, dc)
            sent_out.append(copies.start(
                outgoing.at[h, device[0]], out.at[pl.ds(2 * row, 2), chunk(h)], device
            ))
        out[pl.ds(2 * row, 2), chunk(h)] = outgoing[h, row]

    sums[row] = column_sum
    sums_out = [copies.start(sums.at[row], sums.at[row], in_row(*p)) for p in rows]
    for copy in sums_out:
        copy.wait_recv()
    total = sums[0] + sums[1] + sums[2] + sums[3]
    totals[...] = jnp.broadcast_to(jnp.sum(total, axis=0, keepdims=True), (8, TILE))
    for copy in sent_out:
        copy.wait_recv()
    copies.finish()


def on_device(matrix_tiles, tile_rows, keep_rows, owners):
    meta = jnp.concatenate([tile_rows[0, 0], keep_rows[0, 0]])
    meta = jnp.broadcast_to(jnp.pad(meta, (0, 120))[None], (8, 128))
    f32, bf16 = jnp.float32, jnp.bfloat16
    arrived, totals = pl.pallas_call(
        kernel,
        out_shape=(
            jax.ShapeDtypeStruct((8, TILE, TILE), f32),
            jax.ShapeDtypeStruct((8, TILE), f32),
        ),
        in_specs=[
            pl.BlockSpec(memory_space=pl.ANY),
            pl.BlockSpec(memory_space=pltpu.VMEM),
            pl.BlockSpec(memory_space=pltpu.SMEM),
        ],
        out_specs=[pl.BlockSpec(memory_space=pltpu.VMEM)] * 2,
        scratch_shapes=[
            pltpu.VMEM((8, 8, 128), jnp.int32),
            pltpu.VMEM((4, 4, 8, 128), jnp.int32),
            pltpu.SMEM((8, 8, 128), jnp.int32),
            pltpu.SMEM((4, 4, 8, 128), jnp.int32),
            pltpu.SMEM((64,), jnp.int32),
            pltpu.VMEM((CHUNKS, 8, 4, ROWS, TILE), f32),
            pltpu.VMEM((33, ROWS, TILE), bf16),
            pltpu.VMEM((33, ROWS, TILE), bf16),
            pltpu.VMEM((4, 2, TILE, TILE), f32),
            pltpu.VMEM((4, 4, TILE, TILE), f32),
            pltpu.VMEM((16, TILE, TILE), bf16),
            pltpu.VMEM((16, TILE, TILE), bf16),
            pltpu.VMEM((CHUNKS, 4, 4, ROWS, TILE), f32),
            pltpu.VMEM((CHUNKS, 2, 2, ROWS, TILE), f32),
            pltpu.VMEM((CHUNKS, 2, 4, ROWS, TILE), f32),
            pltpu.VMEM((5, ROWS, TILE), f32),
            pltpu.VMEM((CHUNKS, 4, 2, ROWS, TILE), f32),
            pltpu.VMEM((4, 8, TILE), f32),
            pltpu.SemaphoreType.DMA((REMOTE,)),
            pltpu.SemaphoreType.DMA((REMOTE,)),
            pltpu.SemaphoreType.DMA((LOCAL,)),
        ],
        compiler_params=pltpu.CompilerParams(
            collective_id=0, has_side_effects=True, vmem_limit_bytes=56 << 20
        ),
        name="expand",
    )(matrix_tiles[0, 0], meta, owners[0, :, 0])
    order = float(matrix_tiles.shape[3] * 32)
    owned = order * arrived / totals[0][None, None, :]
    return owned[None, None]


def solution(mesh):
    placed = (
        P("row", "col", None, None, None),
        P("row", "col", None),
        P("row", "col", None),
        P("row", "col", None),
    )
    return jax.shard_map(
        on_device,
        mesh=mesh,
        in_specs=placed,
        out_specs=P("row", "col", None, None, None),
        check_vma=False,
    )
```

```python
import functools

import jax
import jax.numpy as jnp
from jax import lax
from jax.experimental import pallas as pl
from jax.experimental.pallas import tpu as pltpu
from jax.sharding import PartitionSpec as P

MESH = pl.DeviceIdType.MESH
TILE = 256
TR = 8
SIZES = (64, 64, 64, 64)
CHUNKS = len(SIZES)
STARTS = tuple(sum(SIZES[:h]) for h in range(CHUNKS))
MOST = max(SIZES)
PIECES = 4
DONE = 32
ORDER = (
    "own 0",
    "own_across 0",
    "b_column 0",
    "own 1",
    "b_column 1",
    "b_column 2",
    "b_column 3",
    "own_across 1",
    "own_across 2",
    "own_across 3",
    "meta",
    "clear",
    "slots",
    "pass_own 0",
    "across 0",
    "own 2",
    "pass_own 1",
    "b_to_planes 0",
    "own 3",
    "b_to_planes 1",
    "pass_across 0",
    "b_to_planes 2",
    "pass_own 2",
    "places",
    "b_to_planes 3",
    "b_to_core 0",
    "b_to_core 1",
    "b_to_core 2",
    "pass_own 3",
    "across 1",
    "b_to_core 3",
    "across 2",
    "b_split",
    "pass_across 1",
    "split 0",
    "far 0",
    "next 0",
    "last 0",
    "across 3",
    "near 0",
    "pass_across 2",
    "split 1",
    "far 1",
    "next 1",
    "last 1",
    "finish 0",
    "near 1",
    "pass_across 3",
    "split 2",
    "far 2",
    "next 2",
    "last 2",
    "finish 1",
    "near 2",
    "split 3",
    "far 3",
    "next 3",
    "last 3",
    "finish 2",
    "near 3",
    "finish 3",
)


class Copies:
    def __init__(self, send_sems, recv_sems):
        self.send_sems, self.recv_sems, self.made = send_sems, recv_sems, []

    def start(self, src, dst, device):
        number = len(self.made)
        copy = pltpu.make_async_remote_copy(
            src_ref=src,
            dst_ref=dst,
            send_sem=self.send_sems.at[number],
            recv_sem=self.recv_sems.at[number],
            device_id=device,
            device_id_type=MESH,
        )
        copy.start()
        self.made.append(copy)
        return copy

    def finish(self):
        for copy in self.made:
            copy.wait_send()


REMOTE = 3 + 7 + 3 + PIECES * (3 + 3 + 4) + CHUNKS * (9 + 4 + 3) + 3
LOCAL = 1 + CHUNKS + PIECES * 2 + 2


def kernel(
    tiles, tile_rows, keep_rows, owners, out, totals,
    meta, plane_meta, column_meta, plane_scalars, column_scalars, places,
    a_land, a_hi, a_lo, b_own, b_land, b_hi, b_lo,
    partial, near, inflated, outgoing, sums,
    send_sems, recv_sems, local_sems,
):
    row, col = lax.axis_index("row"), lax.axis_index("col")
    yl, core = row // 2, row % 2
    z, yh, x = col // 8, (col // 4) % 2, col % 4
    mine = yh * 4 + x

    def in_plane(dy, dx):
        return (row, z * 8 + ((yh + dy) % 2) * 4 + (x + dx) % 4)

    def in_row(dyl, dc):
        return (((yl + dyl) % 2) * 2 + (core + dc) % 2, col)

    def in_z(d):
        return (row, ((z + d) % 4) * 8 + mine)

    plane = [(dy, dx) for dy in range(2) for dx in range(4) if (dy, dx) != (0, 0)]
    rows = [(0, 1), (1, 0), (1, 1)]
    partners = [in_plane(*p) for p in plane] + [in_row(*p) for p in rows] + [in_z(d) for d in (1, 2, 3)]
    barrier = pltpu.get_barrier_semaphore()
    for device in partners:
        pl.semaphore_signal(barrier, inc=1, device_id=device, device_id_type=MESH)
    pl.semaphore_wait(barrier, len(partners))

    copies = Copies(send_sems, recv_sems)
    local_count = [0]

    def local(src, dst):
        copy = pltpu.make_async_copy(src, dst, local_sems.at[local_count[0]])
        local_count[0] += 1
        copy.start()
        return copy

    right, left, across = in_plane(0, 1), in_plane(0, 3), in_plane(1, 0)
    b_right, b_left = yh * 4 + (x + 1) % 4, yh * 4 + (x + 3) % 4
    b_across = (1 - yh) * 4 + x
    b_across_right, b_across_left = (1 - yh) * 4 + (x + 1) % 4, (1 - yh) * 4 + (x + 3) % 4

    def chunk(h):
        return pl.ds(STARTS[h], SIZES[h])

    a = [dict() for _ in range(CHUNKS)]

    def land(h, block, tiles_of=slice(None)):
        return a_land.at[block, tiles_of, chunk(h)]

    def a_own(h):
        src = tiles.at[:, chunk(h)]
        a[h]["right"] = copies.start(src, land(h, mine), right)
        a[h]["left"] = copies.start(src, land(h, mine), left)
        a[h]["self"] = local(src, land(h, mine))

    def a_own_across(h):
        a[h]["across"] = copies.start(tiles.at[:, chunk(h)], land(h, mine), across)

    def a_pass_own(h):
        a[h]["right"].wait_recv()
        block = land(h, b_left, pl.ds(0, 2))
        a[h]["right2"] = copies.start(block, block, right)
        a[h]["left"].wait_recv()
        block = land(h, b_right, pl.ds(2, 2))
        a[h]["left2"] = copies.start(block, block, left)

    def a_across(h):
        a[h]["across"].wait_recv()
        block = land(h, b_across)
        a[h]["aright"] = copies.start(block, block, right)
        a[h]["aleft"] = copies.start(block, block, left)

    def a_pass_across(h):
        a[h]["aright"].wait_recv()
        block = land(h, b_across_left, pl.ds(0, 2))
        a[h]["aright2"] = copies.start(block, block, right)
        a[h]["aleft"].wait_recv()
        block = land(h, b_across_right, pl.ds(2, 2))
        a[h]["aleft2"] = copies.start(block, block, left)

    def a_ready(h):
        a[h]["self"].wait()
        for name in ("right2", "left2", "aright2", "aleft2"):
            a[h][name].wait_recv()

    meta[0:1, 0:4] = tile_rows[...]
    meta[1:2, 0:4] = keep_rows[...]
    own_meta = local(meta, column_meta.at[z, row])
    meta_row = [copies.start(meta, column_meta.at[z, row], in_row(*p)) for p in rows]
    meta_plane = [copies.start(meta, plane_meta.at[mine], in_plane(*p)) for p in plane]
    plane_meta[mine] = meta[...]

    depth = TILE // PIECES
    b_row, b_self, b_z, b_here, b_share, meta_z = [], [], [], [], [], []

    def b_column(p):
        piece = pl.ds(p * depth, depth)
        b_row.append([
            copies.start(
                tiles.at[pl.ds(2 * ((core + dc) % 2), 2), piece], b_own.at[row, :, piece], in_row(dyl, dc)
            )
            for dyl, dc in rows
        ])
        b_self.append(local(tiles.at[pl.ds(2 * core, 2), piece], b_own.at[row, :, piece]))

    def b_place(plane_of, p):
        return b_land.at[plane_of, pl.ds(2 * core, 2), pl.ds(p * depth, depth)]

    def b_to_planes(p):
        piece = pl.ds(p * depth, depth)
        for copy in b_row[p]:
            copy.wait_recv()
        b_self[p].wait()
        b_z.append([
            copies.start(b_own.at[(z + d) % 4, :, piece], b_place(z, p), in_z(d)) for d in (2, 1, 3)
        ])
        b_here.append(local(b_own.at[z, :, piece], b_place(z, p)))

    def b_to_core(p):
        b_here[p].wait()
        b_share.append(copies.start(b_place(z, p), b_place(z, p), in_row(0, 1)))
        for copy, d in zip(b_z[p], (2, 1, 3)):
            copy.wait_recv()
            block = b_place((z + 4 - d) % 4, p)
            b_share.append(copies.start(block, block, in_row(0, 1)))

    def b_split():
        for copy in b_share:
            copy.wait_recv()
        for d in range(4):
            for slot in range(4):
                value = b_land[(z + d) % 4, slot]
                high = value.astype(jnp.bfloat16)
                b_hi[d * 4 + slot] = high
                b_lo[d * 4 + slot] = (value - high.astype(jnp.float32)).astype(jnp.bfloat16)

    def find_places():
        for copy in meta_plane + meta_z:
            copy.wait_recv()
        to_scalars = [local(plane_meta, plane_scalars), local(column_meta, column_scalars)]
        for copy in to_scalars:
            copy.wait()
        for d in range(4):
            zc = (z + d) % 4
            for slot in range(4):
                level = column_scalars[zc, z, 0, slot]
                for m in range(4):
                    keep = column_scalars[zc, row, 1, m]
                    place = jnp.int32(DONE)
                    for t in range(4):
                        found = plane_scalars[level, 0, t] == keep
                        place = jnp.where(found, level * 4 + t, place)
                    places[(d * 4 + slot) * 4 + m] = place

    def meta_to_planes():
        own_meta.wait()
        for copy in meta_row:
            copy.wait_recv()
        for d in (1, 2, 3):
            meta_z.append(copies.start(column_meta.at[z], column_meta.at[z], in_z(d)))

    def products(h, d):
        size = SIZES[h]
        total = jnp.zeros((4 * size, TILE), jnp.float32)
        for slot in range(4):
            where = [places[(d * 4 + slot) * 4 + m] for m in range(4)]
            high = jnp.concatenate([a_hi[w, 0:size] for w in where], axis=0)
            low = jnp.concatenate([a_lo[w, 0:size] for w in where], axis=0)
            right_high, right_low = b_hi[d * 4 + slot], b_lo[d * 4 + slot]
            total += jnp.dot(high, right_high, preferred_element_type=jnp.float32)
            total += jnp.dot(low, right_high, preferred_element_type=jnp.float32)
            total += jnp.dot(high, right_low, preferred_element_type=jnp.float32)
        partial[d, :, chunk(h)] = total.reshape(4, size, TILE)

    slots, sent_out, column_sums = [], [], []
    c = [dict() for _ in range(CHUNKS)]

    def find_slots():
        for owner in range(4):
            first, second = jnp.int32(4), jnp.int32(4)
            for m in (3, 2, 1, 0):
                hit = owners[m] == owner
                second = jnp.where(hit, first, second)
                first = jnp.where(hit, m, first)
            slots.extend([first, second])

    def clear():
        a_hi[DONE] = jnp.zeros((MOST, TILE), jnp.bfloat16)
        a_lo[DONE] = jnp.zeros((MOST, TILE), jnp.bfloat16)
        inflated[4] = jnp.zeros((MOST, TILE), jnp.float32)

    def a_split(h):
        a_ready(h)
        for b in range(TR):
            for t in range(4):
                value = a_land[b, t, chunk(h)]
                high = value.astype(jnp.bfloat16)
                a_hi[b * 4 + t, 0:SIZES[h]] = high
                a_lo[b * 4 + t, 0:SIZES[h]] = (value - high.astype(jnp.float32)).astype(jnp.bfloat16)

    def c_send(h, d):
        products(h, d)
        c[h][d] = copies.start(partial.at[d, :, chunk(h)], near.at[{1: 0, 3: 1, 2: 2}[d], :, chunk(h)], in_z(d))

    def c_far(h):
        products(h, 2)
        here = chunk(h)
        c[h]["up"] = copies.start(partial.at[2, pl.ds(0, 2), here], near.at[2, pl.ds(0, 2), here], in_z(1))
        c[h]["down"] = copies.start(partial.at[2, pl.ds(2, 2), here], near.at[2, pl.ds(2, 2), here], in_z(3))

    def c_next(h):
        products(h, 1)
        products(h, 3)

    def c_near(h):
        here = chunk(h)
        c[h]["up"].wait_recv()
        partial[1, 0:2, here] = partial[1, 0:2, here] + near[2, 0:2, here]
        c[h][1] = copies.start(partial.at[1, :, here], near.at[0, :, here], in_z(1))
        c[h]["down"].wait_recv()
        partial[3, 2:4, here] = partial[3, 2:4, here] + near[2, 2:4, here]
        c[h][3] = copies.start(partial.at[3, :, here], near.at[1, :, here], in_z(3))

    def c_own(h):
        products(h, 0)

    def c_finish(h):
        size, here = SIZES[h], chunk(h)
        for d in (1, 3, 2):
            if d in c[h]:
                c[h][d].wait_recv()
        column_sum = jnp.zeros((8, TILE), jnp.float32)
        for m in range(4):
            value = partial[0, m, here] + near[0, m, here] + near[1, m, here]
            if 2 in c[h]:
                value = value + near[2, m, here]
            value = value * value
            inflated[m, 0:size] = value
            column_sum = column_sum + jnp.sum(value.reshape(size // 8, 8, TILE), axis=0)
        column_sums.append(column_sum)
        for owner in range(4):
            for n in range(2):
                outgoing[owner, n, here] = inflated[slots[owner * 2 + n], 0:size]
        for dyl, dc in rows:
            device = in_row(dyl, dc)
            sent_out.append(copies.start(
                outgoing.at[device[0], :, here], out.at[pl.ds(2 * row, 2), here], device
            ))
        out[pl.ds(2 * row, 2), here] = outgoing[row, :, here]

    steps = dict(
        own=a_own, own_across=a_own_across, pass_own=a_pass_own, across=a_across, pass_across=a_pass_across,
        b_column=b_column, b_to_planes=b_to_planes, b_to_core=b_to_core, b_split=b_split, meta=meta_to_planes,
        places=find_places, slots=find_slots, clear=clear,
        split=a_split, send=c_send, far=c_far, next=c_next, near=c_near, last=c_own, finish=c_finish,
    )
    for step_of in ORDER:
        name, *numbers = step_of.split()
        steps[name](*[int(n) for n in numbers])

    sums[row] = functools.reduce(jnp.add, column_sums)
    sums_out = [copies.start(sums.at[row], sums.at[row], in_row(*p)) for p in rows]
    for copy in sums_out:
        copy.wait_recv()
    total = sums[0] + sums[1] + sums[2] + sums[3]
    totals[...] = jnp.sum(total, axis=0, keepdims=True)
    for copy in sent_out:
        copy.wait_recv()
    copies.finish()


def on_device(matrix_tiles, tile_rows, keep_rows, owners):
    f32, bf16 = jnp.float32, jnp.bfloat16
    arrived, totals = pl.pallas_call(
        kernel,
        out_shape=(
            jax.ShapeDtypeStruct((8, TILE, TILE), f32),
            jax.ShapeDtypeStruct((1, TILE), f32),
        ),
        in_specs=[
            pl.BlockSpec(memory_space=pl.ANY),
            pl.BlockSpec(memory_space=pltpu.VMEM),
            pl.BlockSpec(memory_space=pltpu.VMEM),
            pl.BlockSpec(memory_space=pltpu.SMEM),
        ],
        out_specs=[pl.BlockSpec(memory_space=pltpu.VMEM)] * 2,
        scratch_shapes=[
            pltpu.VMEM((8, 128), jnp.int32),
            pltpu.VMEM((8, 8, 128), jnp.int32),
            pltpu.VMEM((4, 4, 8, 128), jnp.int32),
            pltpu.SMEM((8, 8, 128), jnp.int32),
            pltpu.SMEM((4, 4, 8, 128), jnp.int32),
            pltpu.SMEM((64,), jnp.int32),
            pltpu.VMEM((8, 4, TILE, TILE), f32),
            pltpu.VMEM((33, MOST, TILE), bf16),
            pltpu.VMEM((33, MOST, TILE), bf16),
            pltpu.VMEM((4, 2, TILE, TILE), f32),
            pltpu.VMEM((4, 4, TILE, TILE), f32),
            pltpu.VMEM((16, TILE, TILE), bf16),
            pltpu.VMEM((16, TILE, TILE), bf16),
            pltpu.VMEM((4, 4, TILE, TILE), f32),
            pltpu.VMEM((3, 4, TILE, TILE), f32),
            pltpu.VMEM((5, MOST, TILE), f32),
            pltpu.VMEM((4, 2, TILE, TILE), f32),
            pltpu.VMEM((4, 8, TILE), f32),
            pltpu.SemaphoreType.DMA((REMOTE,)),
            pltpu.SemaphoreType.DMA((REMOTE,)),
            pltpu.SemaphoreType.DMA((LOCAL,)),
        ],
        compiler_params=pltpu.CompilerParams(
            collective_id=0, has_side_effects=True, vmem_limit_bytes=56 << 20
        ),
        name="expand",
    )(matrix_tiles[0, 0], tile_rows[0], keep_rows[0], owners[0, :, 0])
    order = float(matrix_tiles.shape[3] * 32)
    owned = order * arrived / totals[0][None, None, :]
    return owned[None, None]


def solution(mesh):
    placed = (
        P("row", "col", None, None, None),
        P("row", "col", None),
        P("row", "col", None),
        P("row", "col", None),
    )
    return jax.shard_map(
        on_device,
        mesh=mesh,
        in_specs=placed,
        out_specs=P("row", "col", None, None, None),
        check_vma=False,
    )
```
